32 devices in a mesh: section: 4 (over z), sp: 8 (over y, x, core).
Axes of the slice: x: 2, y: 2, z: 4, core: 2. Of those that a mesh axis runs over, the one named last changes fastest.
Arguments:
- queries: bfloat16 [4, 2, 6, 512, 32, 128], P('section', None, None, 'sp'), may hold values from -400 to 400
- keys: bfloat16 [4, 2, 6, 512, 4, 128], P('section', None, None, 'sp'), may hold values from -31 to 31
- values: bfloat16 [4, 2, 6, 512, 4, 128], P('section', None, None, 'sp'), may hold values from -6 to 6
- top_grad: bfloat16 [2, 6, 512, 32, 128], P(None, None, 'sp'), may hold values from -6 to 6
- head_live: int32 [32], replicated, may hold values 0 or 1
Outputs:
- input_grad: bfloat16 [4, 2, 6, 512, 32, 128], P('section', None, None, 'sp')
- key_grad: float32 [4, 2, 6, 512, 4, 128], P('section', None, None, 'sp')
- value_grad: float32 [4, 2, 6, 512, 4, 128], P('section', None, None, 'sp')
The draws below stay inside these ranges and needn't reach their ends.
All inputs are finite; a program needn't handle non-finite values.
Results may differ from the reference program's by a relative error of at most 0.01.
Values may be sent and summed in bfloat16 or wider, within the bound.
A program may use at most 128 MiB of HBM per device.

```python
import jax
import jax.numpy as jnp
from jax import lax

QH = 32
KVH = 4
HD = 128
SPAN = 512
NCH = 6
SEQS = 2
LAYERS = 4


def shared_draw(key):
    folded = jax.random.fold_in(key, 7)
    key_q, key_k = jax.random.split(folded, 2)
    length_all = NCH * SPAN
    query_draw = jax.random.truncated_normal(key_q, -6.0, 6.0, (LAYERS, SEQS, length_all, QH, HD), jnp.float32)
    key_draw = jax.random.truncated_normal(key_k, -6.0, 6.0, (LAYERS, SEQS, length_all, KVH, HD), jnp.float32)
    return (query_draw.reshape(LAYERS, SEQS, NCH, SPAN, QH, HD), key_draw.reshape(LAYERS, SEQS, NCH, SPAN, KVH, HD))


def draw_queries(key, part):
    return shared_draw(key)[0].astype(jnp.bfloat16)


def draw_keys(key, part):
    return shared_draw(key)[1].astype(jnp.bfloat16)


def place_ends(result, own_key, low, top_value):
    dims = result.shape
    spot = [jax.random.randint(jax.random.fold_in(own_key, axis), (), 0, dims[axis]) for axis in range(len(dims))]
    result = result.at[tuple(spot)].set(low)
    longest = dims.index(max(dims))
    spot[longest] = (spot[longest] + 1) % dims[longest]
    return result.at[tuple(spot)].set(top_value)


def levels(key, extent, pieces, smallest, high):
    def one(dim, shards_of):
        steps = jax.random.uniform(jax.random.fold_in(jax.random.fold_in(key, 6), dim), (shards_of,), jnp.float32, smallest / len(pieces), high / len(pieces))
        return jnp.repeat(jnp.exp(steps), extent[dim] // shards_of).reshape((-1,) + (1,) * (len(extent) - dim - 1))

    factor_of = one(*pieces[0])
    for cut in pieces[1:]:
        factor_of = factor_of * one(*cut)
    return factor_of


def centred(key, dims, deviation, limit, shards=(), dtype=jnp.bfloat16):
    level = levels(key, dims, shards, -0.22, 0.18) if shards else 1.0
    result = jax.random.normal(key, dims, jnp.float32) * deviation * level
    return jnp.minimum(jnp.maximum(result, -limit), limit).astype(dtype)


def setup_inputs(seed: int = 0) -> dict:
    key_of = jax.random.split(jax.random.key(seed), 6)
    return {
        "queries": draw_queries(jax.random.fold_in(key_of[5], 71), 0),
        "keys": draw_keys(jax.random.fold_in(key_of[5], 71), 0),
        "values": centred(key_of[2], (LAYERS, SEQS, NCH, SPAN, KVH, HD), 1.0, 6.0, ((0, 4), (3, 8))),
        "top_grad": centred(key_of[3], (SEQS, NCH, SPAN, QH, HD), 1.0, 6.0, ((2, 8),)),
        "head_live": place_ends((jax.random.randint(key_of[4], (QH,), 0, 8) < 7).astype(jnp.int32), jax.random.fold_in(key_of[4], 1), 0, 1),
    }


def head_backward(operands):
    query_h, key_h, value_h, grad_h = operands
    head_width = query_h.shape[-1]
    score_scale = head_width ** -0.5
    query_f = query_h.astype(jnp.float32)
    key_f = key_h.astype(jnp.float32)
    value_f = value_h.astype(jnp.float32)
    grad_f = grad_h.astype(jnp.float32)
    scores = jnp.einsum("sqd,skd->sqk", query_f, key_f) * score_scale
    length_all = scores.shape[1]
    rows_pos = lax.broadcasted_iota(jnp.int32, (length_all, length_all), 0)
    cols_pos = lax.broadcasted_iota(jnp.int32, (length_all, length_all), 1)
    scores = jnp.where((cols_pos <= rows_pos)[None], scores, -jnp.inf)
    prob_vals = jax.nn.softmax(scores, axis=-1)
    dprob_vals = jnp.einsum("sqd,skd->sqk", grad_f, value_f)
    delta = jnp.sum(prob_vals * dprob_vals, axis=-1, keepdims=True)
    dscore = (prob_vals * (dprob_vals - delta) * score_scale).astype(jnp.bfloat16)
    probs_half = prob_vals.astype(jnp.bfloat16)
    dscore = lax.optimization_barrier(dscore).astype(jnp.float32)
    probs_half = lax.optimization_barrier(probs_half).astype(jnp.float32)
    query_grad = jnp.einsum("sqk,skd->sqd", dscore, key_f)
    key_grad = jnp.einsum("sqk,sqd->skd", dscore, query_f)
    value_grad = jnp.einsum("sqk,sqd->skd", probs_half, grad_f)
    return query_grad, key_grad, value_grad


def reference(queries, keys, values, top_grad, head_live):
    layers, seqcount, spans, row_count, headcount, head_width = queries.shape
    kv_count = keys.shape[4]
    group_size = headcount // kv_count
    length_all = spans * row_count
    incoming = top_grad.reshape(seqcount, length_all, headcount, head_width)
    live_scale = head_live.astype(jnp.bfloat16)[None, None, :, None]
    input_list = [None] * layers
    key_list = [None] * layers
    value_list = [None] * layers
    for layer_idx in range(layers - 1, -1, -1):
        query_l = jnp.moveaxis(queries[layer_idx].reshape(seqcount, length_all, headcount, head_width), 2, 0)
        key_l = jnp.repeat(jnp.moveaxis(keys[layer_idx].reshape(seqcount, length_all, kv_count, head_width), 2, 0), group_size, axis=0)
        value_l = jnp.repeat(jnp.moveaxis(values[layer_idx].reshape(seqcount, length_all, kv_count, head_width), 2, 0), group_size, axis=0)
        grad_l = jnp.moveaxis(incoming * live_scale, 2, 0)
        query_grad, key_grad, value_grad = lax.map(head_backward, (query_l, key_l, value_l, grad_l))
        outgoing = (incoming.astype(jnp.float32) + jnp.moveaxis(query_grad, 0, 2)).astype(jnp.bfloat16)
        input_list[layer_idx] = outgoing.reshape(seqcount, spans, row_count, headcount, head_width)
        key_sum = key_grad.reshape(kv_count, group_size, seqcount, length_all, head_width).sum(axis=1)
        value_sum = value_grad.reshape(kv_count, group_size, seqcount, length_all, head_width).sum(axis=1)
        key_list[layer_idx] = jnp.moveaxis(key_sum, 0, 2).reshape(seqcount, spans, row_count, kv_count, head_width)
        value_list[layer_idx] = jnp.moveaxis(value_sum, 0, 2).reshape(seqcount, spans, row_count, kv_count, head_width)
        incoming = outgoing
    return jnp.stack(input_list), jnp.stack(key_list), jnp.stack(value_list)
```

```python
import functools
import math

import jax
import jax.numpy as jnp
from jax import lax
from jax.experimental import pallas as pl
from jax.experimental.pallas import tpu as pltpu
from jax.sharding import PartitionSpec as P

F32 = jnp.float32
BF16 = jnp.bfloat16
SUB = 8
CHUNK = 32
DOT_KEYS = 256


def dot(a, b):
    return jnp.dot(a, b, preferred_element_type=F32)


def fold(block, op):
    return op(block.reshape(block.shape[0] // SUB, SUB, block.shape[1]), axis=0)


def kernel(
    sections, groups, spans, group_size,
    q_ref, top_ref, k_ref, v_ref, live_ref,
    out_ref, kg_ref, vg_ref,
    grads, s_scr, dp_scr, kt_scr, kacc, vacc, send_sem, recv_sem,
):
    group = pl.program_id(0)
    span = pl.program_id(1)
    item = group * spans + span
    items = groups * spans
    section = lax.axis_index("section")
    sp = lax.axis_index("sp")
    sp_count, local_rows, width = k_ref.shape[0], k_ref.shape[3], k_ref.shape[4]
    keys = sp_count * local_rows
    rows = q_ref.shape[1]
    scale = width ** (-0.5)
    log2_scale = scale * math.log2(math.e)
    is_top = section == sections - 1
    below = lax.max(section - 1, 0)
    above = lax.min(section + 1, sections - 1)

    @pl.when(item == 0)
    def _():
        barrier = pltpu.get_barrier_semaphore()

        @pl.when(section > 0)
        def _():
            pl.semaphore_signal(
                barrier, inc=1, device_id={"section": below}, device_id_type=pl.DeviceIdType.MESH
            )

        @pl.when(section < sections - 1)
        def _():
            pl.semaphore_signal(
                barrier, inc=1, device_id={"section": above}, device_id_type=pl.DeviceIdType.MESH
            )

        pl.semaphore_wait(barrier, (section > 0).astype(jnp.int32) + (section < sections - 1).astype(jnp.int32))

    def relay(i):
        return pltpu.make_async_remote_copy(
            src_ref=grads.at[i],
            dst_ref=grads.at[i],
            send_sem=send_sem.at[i],
            recv_sem=recv_sem.at[i],
            device_id={"section": below},
            device_id_type=pl.DeviceIdType.MESH,
        )

    @pl.when(is_top)
    def _():
        grads[item] = top_ref[0]

    @pl.when(jnp.logical_not(is_top))
    def _():
        relay(item).wait_recv()

    incoming = grads[item]
    q_t = q_ref[0].T
    g_t = (incoming.T.astype(F32) * live_ref[0]).astype(BF16)
    kt_scr[span] = k_ref[:, 0, span].reshape(keys, width).T

    def at(kb, start, size):
        return pl.ds(pl.multiple_of(kb * keys + start, size), size)

    def scores_of(kb, top, masked):
        k_blk = k_ref[:, 0, kb].reshape(keys, width)
        v_blk = v_ref[:, 0, kb].reshape(keys, width)
        for start in range(0, keys, DOT_KEYS):
            s = dot(k_blk[start : start + DOT_KEYS], q_t)
            if masked:
                key_pos = lax.broadcasted_iota(jnp.int32, s.shape, 0) + start
                row_pos = lax.broadcasted_iota(jnp.int32, s.shape, 1) // group_size
                s = jnp.where(key_pos <= row_pos + sp * local_rows, s, -jnp.inf)
            s_scr[at(kb, start, DOT_KEYS)] = s
            top = jnp.maximum(top, fold(s, jnp.max))
            dp_scr[at(kb, start, DOT_KEYS)] = dot(v_blk[start : start + DOT_KEYS], g_t)
        return top

    top = scores_of(span, jnp.full((SUB, rows), -jnp.inf, F32), True)
    top = lax.fori_loop(0, span, lambda kb, top: scores_of(kb, top, False), top)
    top = jnp.max(top, axis=0, keepdims=True)

    def weights_of(kb, sums):
        total, weighted = sums
        for start in range(0, keys, CHUNK):
            p = jnp.exp2((s_scr[at(kb, start, CHUNK)] - top) * log2_scale)
            s_scr[at(kb, start, CHUNK)] = p
            total = total + fold(p, jnp.sum)
            weighted = weighted + fold(p * dp_scr[at(kb, start, CHUNK)], jnp.sum)
        return total, weighted

    zero = jnp.zeros((SUB, rows), F32)
    total, weighted = lax.fori_loop(0, span + 1, weights_of, (zero, zero))
    inverse = 1.0 / jnp.sum(total, axis=0, keepdims=True)
    delta = jnp.sum(weighted, axis=0, keepdims=True) * inverse
    q_n = (q_t.astype(F32) * (inverse * scale)).astype(BF16).T
    g_n = (g_t.astype(F32) * inverse).astype(BF16).T

    def grads_of(kb, query_t, first):
        for start in range(0, keys, DOT_KEYS):
            ds, ph = [], []
            for part in range(start, start + DOT_KEYS, CHUNK):
                p = s_scr[at(kb, part, CHUNK)]
                ds.append((p * (dp_scr[at(kb, part, CHUNK)] - delta)).astype(BF16))
                ph.append(p.astype(BF16))
            ds = jnp.concatenate(ds, axis=0)
            ph = jnp.concatenate(ph, axis=0)
            here = pl.ds(start, DOT_KEYS)
            key_part = dot(ds, q_n)
            value_part = dot(ph, g_n)
            if first:
                kacc[kb, here] = key_part
                vacc[kb, here] = value_part
            else:
                kacc[kb, here] += key_part
                vacc[kb, here] += value_part
            query_t = query_t + dot(kt_scr[kb, :, here], ds)
        return query_t

    query_t = grads_of(span, jnp.zeros((width, rows), F32), True)
    query_t = lax.fori_loop(0, span, lambda kb, acc: grads_of(kb, acc, False), query_t)
    query_grad = (query_t * (inverse * scale)).T
    outgoing = (grads[item].astype(F32) + query_grad).astype(BF16)
    out_ref[0] = outgoing
    grads[item] = outgoing

    @pl.when(section > 0)
    def _():
        relay(item).start()

    @pl.when(span == spans - 1)
    def _():
        for kb in range(spans):
            kg_ref[:, 0, kb] = kacc[kb].astype(BF16).reshape(sp_count, local_rows, width)
            vg_ref[:, 0, kb] = vacc[kb].astype(BF16).reshape(sp_count, local_rows, width)

    @pl.when(jnp.logical_and(item == items - 1, section > 0))
    def _():
        @pl.loop(0, items)
        def _(i):
            relay(i).wait_send()


def body(queries, keys, values, top_grad, head_live):
    sp_count = lax.axis_size("sp")
    sections = lax.axis_size("section")
    _, seqs, spans, local_rows, heads, width = queries.shape
    kv_count = keys.shape[4]
    group_size = heads // kv_count
    groups = seqs * kv_count
    rows = local_rows * group_size
    items = groups * spans
    full_keys = local_rows * sp_count

    def to_items(x):
        x = x.reshape(seqs, spans, local_rows, kv_count, group_size, width)
        return x.transpose(0, 3, 1, 2, 4, 5).reshape(items, rows, width)

    def gather(x):
        x = x[0].transpose(0, 3, 1, 2, 4).reshape(groups, spans, local_rows, width)
        return lax.all_gather(x, "sp", axis=0, tiled=False)

    key_all, value_all = gather(keys), gather(values)
    q_items, top_items = to_items(queries[0]), to_items(top_grad)
    live = jnp.tile(head_live.astype(F32).reshape(kv_count, 1, group_size), (1, 1, local_rows))

    item_spec = pl.BlockSpec((1, rows, width), lambda a, i: (a * spans + i, 0, 0))
    kv_spec = pl.BlockSpec(
        (sp_count, 1, spans, local_rows, width), lambda a, i: (0, a, 0, 0, 0)
    )
    units = groups * spans * (spans + 1) // 2
    kv_shape = jax.ShapeDtypeStruct((sp_count, groups, spans, local_rows, width), BF16)
    out, key_part, value_part = pl.pallas_call(
        functools.partial(kernel, sections, groups, spans, group_size),
        grid=(groups, spans),
        in_specs=[
            item_spec,
            item_spec,
            kv_spec,
            kv_spec,
            pl.BlockSpec((1, 1, rows), lambda a, i: (a % kv_count, 0, 0)),
        ],
        out_specs=[item_spec, kv_spec, kv_spec],
        out_shape=[jax.ShapeDtypeStruct((items, rows, width), BF16), kv_shape, kv_shape],
        scratch_shapes=[
            pltpu.VMEM((items, rows, width), BF16),
            pltpu.VMEM((spans * full_keys, rows), F32),
            pltpu.VMEM((spans * full_keys, rows), F32),
            pltpu.VMEM((spans, width, full_keys), BF16),
            pltpu.VMEM((spans, full_keys, width), F32),
            pltpu.VMEM((spans, full_keys, width), F32),
            pltpu.SemaphoreType.DMA((items,)),
            pltpu.SemaphoreType.DMA((items,)),
        ],
        compiler_params=pltpu.CompilerParams(
            collective_id=0,
            has_side_effects=True,
            dimension_semantics=("arbitrary", "arbitrary"),
            vmem_limit_bytes=60 * 1024 * 1024,
        ),
        cost_estimate=pl.CostEstimate(
            flops=10 * units * full_keys * rows * width,
            bytes_accessed=8 * items * rows * width,
            transcendentals=units * full_keys * rows,
        ),
        name="span_relay",
    )(q_items, top_items, key_all, value_all, live)

    def scatter(x):
        x = lax.psum_scatter(x, "sp", scatter_dimension=0, tiled=False)
        x = x.reshape(seqs, kv_count, spans, local_rows, width)
        return x.transpose(0, 2, 3, 1, 4).astype(F32)[None]

    key_grad, value_grad = scatter(key_part), scatter(value_part)
    out = out.reshape(seqs, kv_count, spans, local_rows, group_size, width)
    input_grad = out.transpose(0, 2, 3, 1, 4, 5).reshape(queries.shape)
    return input_grad, key_grad, value_grad


def solution(mesh):
    row_spec = P("section", None, None, "sp", None, None)
    return jax.shard_map(
        body,
        mesh=mesh,
        in_specs=(row_spec, row_spec, row_spec, P(None, None, "sp", None, None), P()),
        out_specs=(row_spec, row_spec, row_spec),
        check_vma=False,
    )
```
